32 devices in a mesh: patch: 2 (over y), epoch: 4 (over z), tile: 4 (over x, core).
Axes of the slice: x: 2, y: 2, z: 4, core: 2. Of those that a mesh axis runs over, the one named last changes fastest.
Arguments:
- template: float32 [768, 512], P(('patch', 'epoch'), 'tile'), parts along dimension 0, may hold values from -14.2 to 14.2
- science: float32 [8, 384, 512], P(('patch', 'epoch'), None, 'tile'), parts along dimension 0, may hold values from -31 to 31
- row_profiles: float32 [12, 21], replicated, may hold values from -1.25 to 1.25
- col_profiles: float32 [12, 21], replicated, may hold values from -1.25 to 1.25
- coverage: int32 [8, 256], P(('patch', 'epoch'), 'tile'), parts along dimension 0, may hold values 0 or 1
- stamp_rows: int32 [512], P(('patch', 'tile')), parts along dimension 0, may hold values from 0 to 352
- stamp_cols: int32 [512], P(('patch', 'tile')), parts along dimension 0, may hold values from 0 to 96
Outputs:
- difference: float32 [8, 384, 512], P(('patch', 'epoch'), None, 'tile'), parts along dimension 0
The draws below stay inside these ranges and needn't reach their ends.
There are 2 independent parts, one for each index of `patch`. The reference program is written for one: setup_inputs(seed, part) draws one part's arguments, and reference() takes and returns one part's arrays. A program takes and returns all parts, laid end to end along the dimension named above; an argument that names none is the same for every part. Nothing has to cross between parts.
All inputs are finite; a program needn't handle non-finite values. No bound on the sum of `coverage` on one device may be relied on, other than what follows from the above.
Results may differ from the reference program's by a relative error of at most 0.00011.
Values sent between devices are 32-bit elements; how exact they have to be, the bound alone decides.
A program may use at most 128 MiB of HBM per device.

```python
import jax
import jax.numpy as jnp
from jax import lax

NB = 12
KER = 21
S = 32
NS_TILE = 64
NR = 384
CW = 128
NC = 512
VISITS = 4
NSTAMP = 256


def patch_base(key):
    field = jax.random.normal(jax.random.fold_in(key, 11), (NR, NC), jnp.float32)
    field = jnp.clip(field, -5.0, 5.0)
    return field


def draw_template(key, part):
    return patch_base(key)


def draw_science(key, part):
    field = patch_base(key)
    gains = jnp.exp(jax.random.uniform(jax.random.fold_in(key, 12), (VISITS, 1, 1), jnp.float32, -0.7, 0.7))
    noise = jnp.clip(jax.random.normal(jax.random.fold_in(key, 14), (VISITS, NR, NC), jnp.float32), -5.0, 5.0)
    blended = 0.6 * field + 0.4 * jnp.roll(field, 1, axis=1)
    return gains * blended[None] + 0.3 * noise


def with_ends(drawn, rng, smallest, largest):
    spot = [jax.random.randint(jax.random.fold_in(rng, axis), (), 0, length) for axis, length in enumerate(drawn.shape)]
    longest = drawn.shape.index(max(drawn.shape))
    next_to = spot[:longest] + [(spot[longest] + 1) % drawn.shape[longest]] + spot[longest + 1:]
    return drawn.at[tuple(spot)].set(smallest).at[tuple(next_to)].set(largest)


def bell_draw(key, dims, width, reach, kind=jnp.bfloat16):
    values = jax.random.normal(key, dims, jnp.float32) * width
    return jnp.minimum(jnp.maximum(values, -reach), reach).astype(kind)


def setup_inputs(seed: int = 0, part: int = 0) -> dict:
    seeds = jax.random.split(jax.random.key(seed), 8)
    part_keys = jax.random.split(jax.random.fold_in(seeds[7], part), 8)
    template = draw_template(jax.random.fold_in(jax.random.fold_in(seeds[7], part), 71), part)
    science = draw_science(jax.random.fold_in(jax.random.fold_in(seeds[7], part), 71), part)
    row_profiles = bell_draw(seeds[2], (NB, KER), KER ** -0.5, 1.25, jnp.float32)
    col_profiles = bell_draw(seeds[3], (NB, KER), KER ** -0.5, 1.25, jnp.float32)
    coverage = with_ends((jax.random.randint(part_keys[4], (VISITS, NSTAMP), 0, 4) < 3).astype(jnp.int32), jax.random.fold_in(part_keys[4], 1), 0, 1)
    stamp_rows = with_ends(jax.random.randint(part_keys[5], (NSTAMP,), 0, NR - S + 1), jax.random.fold_in(part_keys[5], 1), 0, NR - S).astype(jnp.int32)
    stamp_cols = with_ends(jax.random.randint(part_keys[6], (NSTAMP,), 0, CW - S + 1), jax.random.fold_in(part_keys[6], 1), 0, CW - S).astype(jnp.int32)
    return dict(template=template, science=science, row_profiles=row_profiles, col_profiles=col_profiles, coverage=coverage, stamp_rows=stamp_rows, stamp_cols=stamp_cols)


ridge_weight = 1.0

def build_features(windows, xi_win, eta_win):
    count = windows.shape[0]
    stacked = jnp.stack([windows, windows * xi_win[:, None, None, :], windows * eta_win[:, None, :, None]], axis=2)
    flattened = stacked.reshape(count, 3 * NB, S * S)
    constant = jnp.ones((count, 1, S * S), jnp.float32)
    return jnp.concatenate([flattened, constant], axis=1)

def reference(template, science, row_profiles, col_profiles, coverage, stamp_rows, stamp_cols):
    half_width = KER // 2
    padded = jnp.pad(template, half_width)
    across = jnp.zeros((NB, NR + 2 * half_width, NC), jnp.float32)
    for offset in range(KER):
        across = across + col_profiles[:, offset][:, None, None] * padded[None, :, offset:offset + NC]
    images = jnp.zeros((NB, NR, NC), jnp.float32)
    for offset in range(KER):
        images = images + row_profiles[:, offset][:, None, None] * across[:, offset:offset + NR, :]
    strip_of = (jnp.arange(NSTAMP) // NS_TILE).astype(jnp.int32)
    global_cols = (strip_of * CW + stamp_cols).astype(jnp.int32)
    zero_index = jnp.zeros((), jnp.int32)
    xi_all = 2.0 * jnp.arange(NC).astype(jnp.float32) / NC - 1.0
    eta_all = 2.0 * jnp.arange(NR).astype(jnp.float32) / NR - 1.0

    def cut_stamp(row_at, col_at):
        return lax.dynamic_slice(images, (zero_index, row_at, col_at), (NB, S, S))
    windows = jax.vmap(cut_stamp)(stamp_rows, global_cols)
    xi_win = jax.vmap(lambda col_at: lax.dynamic_slice_in_dim(xi_all, col_at, S))(global_cols)
    eta_win = jax.vmap(lambda row_at: lax.dynamic_slice_in_dim(eta_all, row_at, S))(stamp_rows)
    features = build_features(windows, xi_win, eta_win)
    stamp_grams = jnp.einsum('sfp,sgp->sfg', features, features, precision=lax.Precision.HIGHEST)
    weights = coverage.astype(jnp.float32)
    grams = jnp.einsum('vs,sfg->vfg', weights, stamp_grams, precision=lax.Precision.HIGHEST)
    unknowns = 3 * NB + 1

    def per_visit(items):
        visit_image, visit_weights, normal_matrix = items
        sci_win = jax.vmap(lambda row_at, col_at: lax.dynamic_slice(visit_image, (row_at, col_at), (S, S)))(stamp_rows, global_cols)
        weighted = features * visit_weights[:, None, None]
        normal_rhs = jnp.einsum('sfp,sp->f', weighted, sci_win.reshape(NSTAMP, S * S), precision=lax.Precision.HIGHEST)
        system = normal_matrix + ridge_weight * jnp.eye(unknowns, dtype=jnp.float32)
        factor = jnp.linalg.cholesky(system)
        coefficients = jax.scipy.linalg.cho_solve((factor, True), normal_rhs)
        per_basis = coefficients[:3 * NB].reshape(NB, 3)
        model_field = jnp.einsum('b,byx->yx', per_basis[:, 0], images, precision=lax.Precision.HIGHEST)
        model_field = model_field + xi_all[None, :] * jnp.einsum('b,byx->yx', per_basis[:, 1], images, precision=lax.Precision.HIGHEST)
        model_field = model_field + eta_all[:, None] * jnp.einsum('b,byx->yx', per_basis[:, 2], images, precision=lax.Precision.HIGHEST)
        model_field = model_field + coefficients[3 * NB]
        return visit_image - model_field
    return lax.map(per_visit, (science, weights, grams))
```

```python
import functools

import jax
import jax.numpy as jnp
from jax import lax
from jax.experimental import pallas as pl
from jax.experimental.pallas import tpu as pltpu
from jax.sharding import PartitionSpec as P

S = 32
GROUP = 16
LANES = 128
ridge_weight = 1.0
F32 = jnp.float32
BF16 = jnp.bfloat16
NT = (((1,), (1,)), ((), ()))
NN = (((1,), (0,)), ((), ()))


def split(value):
    high = value.astype(BF16)
    return high, (value - high.astype(F32)).astype(BF16)


def dot3(left, right, dims):
    left_high, left_low = left
    right_high, right_low = right
    dot = functools.partial(lax.dot_general, dimension_numbers=dims, preferred_element_type=F32)
    return dot(left_high, right_high) + (dot(left_high, right_low) + dot(left_low, right_high))


def toeplitz(profile_row, rows, shift, width):
    base = pltpu.roll(jnp.broadcast_to(profile_row, (8, width)), 0, 1, stride=1, stride_axis=0)
    turns = [(shift + first) % width for first in range(0, rows, 8)]
    return jnp.concatenate([pltpu.roll(base, turn, 1) if turn else base for turn in turns], axis=0)


def iota(shape, axis):
    return lax.broadcasted_iota(jnp.int32, shape, axis)


def row_block(rows, extra, width):
    best = 8
    for size in range(8, width - extra + 1, 8):
        if rows % size == 0:
            best = size
    return best


def xi_row(cols, total):
    start = lax.axis_index("tile") * cols
    return 2.0 * (start + iota((1, cols), 1)).astype(F32) / total - 1.0


def convolve(strip, rowp_ref, colp_ref, images_ref, mixed_ref, taps):
    count, rows, cols = images_ref.shape
    width = 2 * LANES
    half = taps // 2
    block = row_block(rows, taps - 1, width)
    strip = split(strip)
    for b in range(count):
        band = split(toeplitz(colp_ref[b : b + 1, :], cols, -half, width))
        across = dot3(strip, band, NT)
        across = split(across)
        band = split(toeplitz(rowp_ref[b : b + 1, :], block, 0, width))
        for start in range(0, rows, block):
            piece = dot3(band, tuple(part[start : start + width] for part in across), NN)
            images_ref[b, start : start + block, :] = piece
            mixed_ref[pl.ds(start * GROUP + b, block, stride=GROUP), :] = piece


def gram(srow_ref, scol_ref, cov_ref, mixed_ref, rows, cols, total):
    stamps = srow_ref.shape[1]
    at = iota((stamps, cols), 1) - scol_ref[...]
    cols_in = jnp.where((at >= 0) & (at < S), cov_ref[...].astype(F32), 0.0).astype(BF16)
    xi = xi_row(cols, total)
    step = 16
    size = step * GROUP

    def body(chunk, acc):
        y = chunk * step + iota((size, 1), 0) // GROUP
        at_row = y - srow_ref[...]
        rows_in = jnp.where((at_row >= 0) & (at_row < S), 1.0, 0.0).astype(BF16)
        weight = lax.dot_general(rows_in, cols_in, NN, preferred_element_type=F32)
        base = mixed_ref[pl.ds(pl.multiple_of(chunk * size, size), size), :]
        eta = 2.0 * y.astype(F32) / rows - 1.0
        feats = (base, base * xi, base * eta)

        def lay(values):
            return jnp.concatenate(
                [
                    jnp.concatenate([v[k * GROUP : (k + 1) * GROUP] for k in range(step)], axis=1)
                    for v in values
                ],
                axis=0,
            )

        right = split(lay(feats))
        left = split(lay([f * weight for f in feats]))
        return acc + dot3(left, right, NT)

    return lax.fori_loop(0, rows // step, body, jnp.zeros((3 * GROUP, 3 * GROUP), F32))


def solve(normal, count):
    side = 3 * GROUP
    row, col = iota((side, LANES), 0), iota((side, LANES), 1)

    def used(k):
        return ((k % GROUP < count) & (k < side)) | (k == count)

    normal = jnp.concatenate([normal, jnp.zeros((side, LANES - side), F32)], axis=1)
    rhs = normal[:, count + 1 : count + 2]
    system = jnp.where(used(row) & used(col), normal, 0.0) + ridge_weight * jnp.where(row == col, 1.0, 0.0)
    system = jnp.where((col == side) & used(row), rhs, system)
    unknowns = [k for k in range(side) if (k % GROUP < count) or k == count]
    for p in unknowns:
        pivot_row = system[p : p + 1, :]
        factor = system[:, p : p + 1] / system[p : p + 1, p : p + 1]
        factor = jnp.where(row[:, :1] == p, 0.0, factor)
        system = system - factor * pivot_row
    diagonal = jnp.sum(jnp.where(row == col, system, 0.0), axis=1, keepdims=True)
    return system[:, side : side + 1] / diagonal


def apply(coefs, images_ref, science_ref, out_ref, total):
    count, rows, cols = images_ref.shape
    xi = xi_row(cols, total)
    eta = 2.0 * iota((rows, 1), 0).astype(F32) / rows - 1.0
    field = jnp.broadcast_to(coefs[count : count + 1, :], (rows, cols))
    for b in range(count):
        flat = coefs[b : b + 1] + coefs[GROUP + b : GROUP + b + 1] * xi
        field = field + images_ref[b] * (flat + coefs[2 * GROUP + b : 2 * GROUP + b + 1] * eta)
    out_ref[0] = science_ref[0] - field


def fill_rest(mixed_ref, science, count):
    rows = science.shape[0]
    mixed_ref[pl.ds(count, rows, stride=GROUP), :] = jnp.ones_like(science)
    mixed_ref[pl.ds(count + 1, rows, stride=GROUP), :] = science
    for spare in range(count + 2, GROUP):
        mixed_ref[pl.ds(spare, rows, stride=GROUP), :] = jnp.zeros_like(science)


def front(taps, total, strip_ref, side_ref, science_ref, rowp_ref, colp_ref, cov_ref, srow_ref, scol_ref,
          images_ref, gram_ref, mixed_ref):
    count, rows, cols = images_ref.shape
    fill_rest(mixed_ref, science_ref[0], count)
    strip = jnp.concatenate([strip_ref[...], side_ref[...]], axis=1)
    convolve(strip, rowp_ref, colp_ref, images_ref, mixed_ref, taps)
    gram_ref[...] = gram(srow_ref, scol_ref, cov_ref, mixed_ref, rows, cols, total)


def back(total, gram_ref, images_ref, science_ref, out_ref):
    coefs = solve(gram_ref[...], images_ref.shape[0])
    apply(coefs, images_ref, science_ref, out_ref, total)


def local(template, science, row_profiles, col_profiles, coverage, stamp_rows, stamp_cols):
    count, taps = row_profiles.shape
    half = taps // 2
    rows, cols = science.shape[1:]
    tiles = lax.axis_size("tile")
    total = cols * tiles
    width = 2 * LANES
    block = row_block(rows, taps - 1, width)
    high = rows - block + width
    column = lax.all_gather(template, "epoch", axis=0, tiled=True)
    right = lax.ppermute(column[:, :half], "tile", [(i + 1, i) for i in range(tiles - 1)])
    left = lax.ppermute(column[:, cols - half :], "tile", [(i, i + 1) for i in range(tiles - 1)])
    side = jnp.concatenate([right, jnp.zeros((rows, LANES - 2 * half), F32), left], axis=1)
    pads = ((half, high - rows - half), (0, 0))
    fit = ((0, 0), (0, width - taps))
    vmem = pl.BlockSpec(memory_space=pltpu.VMEM)
    images, normal = pl.pallas_call(
        functools.partial(front, taps, total),
        out_shape=(
            jax.ShapeDtypeStruct((count, rows, cols), F32),
            jax.ShapeDtypeStruct((3 * GROUP, 3 * GROUP), F32),
        ),
        in_specs=[vmem] * 8,
        out_specs=(vmem, vmem),
        scratch_shapes=[pltpu.VMEM((rows * GROUP, cols), F32)],
        compiler_params=pltpu.CompilerParams(vmem_limit_bytes=48 * 2**20),
    )(
        jnp.pad(column, pads),
        jnp.pad(side, pads),
        science,
        jnp.pad(row_profiles, fit),
        jnp.pad(col_profiles, fit),
        coverage.reshape(-1, 1),
        stamp_rows.reshape(1, -1),
        stamp_cols.reshape(-1, 1),
    )
    normal = lax.psum(normal, "tile")
    return pl.pallas_call(
        functools.partial(back, total),
        out_shape=jax.ShapeDtypeStruct(science.shape, F32),
        in_specs=[vmem] * 3,
        out_specs=vmem,
        compiler_params=pltpu.CompilerParams(vmem_limit_bytes=48 * 2**20),
    )(normal, images, science)


def solution(mesh):
    in_specs = (
        P(("patch", "epoch"), "tile"),
        P(("patch", "epoch"), None, "tile"),
        P(),
        P(),
        P(("patch", "epoch"), "tile"),
        P(("patch", "tile")),
        P(("patch", "tile")),
    )
    out_specs = P(("patch", "epoch"), None, "tile")
    return jax.shard_map(local, mesh=mesh, in_specs=in_specs, out_specs=out_specs, check_vma=False)
```

```python
import functools

import jax
import jax.numpy as jnp
from jax import lax
from jax.experimental import pallas as pl
from jax.experimental.pallas import tpu as pltpu
from jax.sharding import PartitionSpec as P

S = 32
GROUP = 16
EDGE = 16
CHUNK = 16
LANES = 128
ridge_weight = 1.0
F32 = jnp.float32
BF16 = jnp.bfloat16
NT = (((1,), (1,)), ((), ()))
NN = (((1,), (0,)), ((), ()))


def split(value):
    high = value.astype(BF16)
    return high, (value - high.astype(F32)).astype(BF16)


def dot3(left, right, dims):
    left_high, left_low = left
    right_high, right_low = right
    dot = functools.partial(lax.dot_general, dimension_numbers=dims, preferred_element_type=F32)
    return dot(left_high, right_high) + (dot(left_high, right_low) + dot(left_low, right_high))


def toeplitz(profile_row, rows, shift, width):
    base = pltpu.roll(jnp.broadcast_to(profile_row, (8, width)), 0, 1, stride=1, stride_axis=0)
    turns = [(shift + first) % width for first in range(0, rows, 8)]
    return jnp.concatenate([pltpu.roll(base, turn, 1) if turn else base for turn in turns], axis=0)


def iota(shape, axis):
    return lax.broadcasted_iota(jnp.int32, shape, axis)


def row_block(rows, extra, width):
    best = 8
    for size in range(8, width - extra + 1, 8):
        if rows % size == 0:
            best = size
    return best


def xi_row(cols, total):
    start = lax.axis_index("tile") * cols
    return 2.0 * (start + iota((1, cols), 1)).astype(F32) / total - 1.0


def make_bands(rowp_ref, colp_ref, profile_ref, row_band_ref, col_band_ref, shift):
    count, taps = rowp_ref.shape
    width = profile_ref.shape[2]
    profile_ref[...] = jnp.zeros_like(profile_ref)
    profile_ref[0, :count, :taps] = rowp_ref[...]
    profile_ref[1, :count, :taps] = colp_ref[...]
    for b in range(count):
        band = split(toeplitz(profile_ref[0, b : b + 1, :], row_band_ref.shape[2], shift, width))
        row_band_ref[0, b], row_band_ref[1, b] = band
        band = split(toeplitz(profile_ref[1, b : b + 1, :], col_band_ref.shape[2], -(taps // 2), width))
        col_band_ref[0, b], col_band_ref[1, b] = band


def convolve(strip, row_band_ref, col_band_ref, images_ref, mixed_ref):
    count, rows, cols = images_ref.shape
    block, width = row_band_ref.shape[2:]
    strip = split(strip)
    for b in range(count):
        across = dot3(strip, (col_band_ref[0, b], col_band_ref[1, b]), NT)
        across = split(across)
        band = (row_band_ref[0, b], row_band_ref[1, b])
        for start in range(0, rows, block):
            piece = dot3(band, tuple(part[start : start + width] for part in across), NN)
            images_ref[b, start : start + block, :] = piece
            mixed_ref[pl.ds(start * GROUP + b, block, stride=GROUP), :] = piece


def make_weight(srow_ref, scol_ref, cov_ref, weight_ref):
    cols = weight_ref.shape[1]
    stamps = srow_ref.shape[1]
    at = iota((cols, stamps), 0) - scol_ref[...]
    cols_in = jnp.where((at >= 0) & (at < S), cov_ref[...].astype(F32), 0.0).astype(BF16)
    size = CHUNK * GROUP

    def body(chunk, carry):
        at_row = chunk * CHUNK + iota((size, 1), 0) // GROUP - srow_ref[...]
        rows_in = jnp.where((at_row >= 0) & (at_row < S), 1.0, 0.0).astype(BF16)
        at = pl.ds(pl.multiple_of(chunk * size, size), size)
        weight_ref[at, :] = lax.dot_general(rows_in, cols_in, NT, preferred_element_type=F32)
        return carry

    lax.fori_loop(0, weight_ref.shape[0] // size, body, 0)


def gram(weight_ref, mixed_ref, total):
    height, cols = mixed_ref.shape
    rows = height // GROUP
    xi = xi_row(cols, total)
    size = CHUNK * GROUP

    def lay(values):
        return jnp.concatenate(
            [
                jnp.concatenate([v[k * GROUP : (k + 1) * GROUP] for k in range(CHUNK)], axis=1)
                for v in values
            ],
            axis=0,
        )

    def body(chunk, acc):
        at = pl.ds(pl.multiple_of(chunk * size, size), size)
        base = mixed_ref[at, :]
        weight = weight_ref[at, :]
        y = chunk * CHUNK + iota((size, 1), 0) // GROUP
        eta = 2.0 * y.astype(F32) / rows - 1.0
        feats = (base, base * xi, base * eta)
        right = split(lay(feats))
        left = split(lay([f * weight for f in feats]))
        return acc + dot3(left, right, NT)

    return lax.fori_loop(0, rows // CHUNK, body, jnp.zeros((3 * GROUP, 3 * GROUP), F32))


def solve(normal, count):
    side = 3 * GROUP
    row, col = iota((side, LANES), 0), iota((side, LANES), 1)

    def used(k):
        return ((k % GROUP < count) & (k < side)) | (k == count)

    rhs = normal[:, count + 1 : count + 2]
    system = jnp.where(used(row) & used(col), normal, 0.0) + ridge_weight * jnp.where(row == col, 1.0, 0.0)
    system = jnp.where((col == side) & used(row), rhs, system)
    unknowns = [k for k in range(side) if (k % GROUP < count) or k == count]
    for p in unknowns:
        pivot_row = system[p : p + 1, :]
        factor = system[:, p : p + 1] / system[p : p + 1, p : p + 1]
        factor = jnp.where(row[:, :1] == p, 0.0, factor)
        system = system - factor * pivot_row
    diagonal = jnp.sum(jnp.where(row == col, system, 0.0), axis=1, keepdims=True)
    return system[:, side : side + 1] / diagonal


def apply(coefs, images_ref, science_ref, out_ref, total):
    count, rows, cols = images_ref.shape
    xi = xi_row(cols, total)
    eta = 2.0 * iota((rows, 1), 0).astype(F32) / rows - 1.0
    field = jnp.broadcast_to(coefs[count : count + 1, :], (rows, cols))
    for b in range(count):
        flat = coefs[b : b + 1] + coefs[GROUP + b : GROUP + b + 1] * xi
        field = field + images_ref[b] * (flat + coefs[2 * GROUP + b : 2 * GROUP + b + 1] * eta)
    out_ref[0] = science_ref[0] - field


def fill_rest(mixed_ref, science, count):
    rows = science.shape[0]
    mixed_ref[pl.ds(count, rows, stride=GROUP), :] = jnp.ones_like(science)
    mixed_ref[pl.ds(count + 1, rows, stride=GROUP), :] = science
    for spare in range(count + 2, GROUP):
        mixed_ref[pl.ds(spare, rows, stride=GROUP), :] = jnp.zeros_like(science)


def remote(source, target, send, recv, epoch, tile):
    return pltpu.make_async_remote_copy(
        src_ref=source,
        dst_ref=target,
        send_sem=send,
        recv_sem=recv,
        device_id={"epoch": epoch, "tile": tile},
        device_id_type=pl.DeviceIdType.MESH,
    )


def kernel(total, top, template_ref, science_ref, rowp_ref, colp_ref, cov_ref, srow_ref, scol_ref, out_ref,
           slots, pack, edges, strip, parts, mine, images_ref, mixed_ref, weight_ref, profile_ref,
           row_band_ref, col_band_ref, slot_send, slot_recv, edge_send, edge_recv, part_send, part_recv):
    count, rows, cols = images_ref.shape
    taps = rowp_ref.shape[1]
    epochs, own_rows, _ = slots.shape
    tiles = parts.shape[0]
    epoch, tile = lax.axis_index("epoch"), lax.axis_index("tile")

    flipped = jnp.transpose(template_ref[...])
    pack[0] = flipped[:EDGE]
    pack[1] = flipped[cols - EDGE :]
    slots[epoch] = template_ref[...]

    barrier = pltpu.get_barrier_semaphore()
    for e in range(epochs):
        for t in range(tiles):
            if e or t:
                where = {"epoch": lax.rem(epoch + e, epochs), "tile": lax.rem(tile + t, tiles)}
                pl.semaphore_signal(barrier, inc=1, device_id=where, device_id_type=pl.DeviceIdType.MESH)
    pl.semaphore_wait(barrier, epochs * tiles - 1)

    def block_copy(e, source):
        return remote(template_ref, slots.at[source], slot_send.at[e], slot_recv.at[source],
                      lax.rem(epoch + e, epochs), tile)

    def edge_copy(e, side, source):
        beside = tile - 1 if side == 0 else tile + 1
        return remote(pack.at[side], edges.at[side, source], edge_send.at[side, e], edge_recv.at[side, source],
                      lax.rem(epoch + e, epochs), beside)

    has_left, has_right = tile > 0, tile < tiles - 1
    order = sorted(range(epochs), key=lambda e: -e * (epochs - e))
    for e in order:
        if e:
            block_copy(e, epoch).start()

        @pl.when(has_left)
        def _():
            edge_copy(e, 0, epoch).start()

        @pl.when(has_right)
        def _():
            edge_copy(e, 1, epoch).start()

    fill_rest(mixed_ref, science_ref[0], count)
    make_weight(srow_ref, scol_ref, cov_ref, weight_ref)
    make_bands(rowp_ref, colp_ref, profile_ref, row_band_ref, col_band_ref, top - taps // 2)
    strip[...] = jnp.zeros_like(strip)

    @pl.when(tile == tiles - 1)
    def _():
        edges[0] = jnp.zeros(edges.shape[1:], F32)

    @pl.when(tile == 0)
    def _():
        edges[1] = jnp.zeros(edges.shape[1:], F32)

    for e in range(epochs):
        source = lax.rem(epoch + epochs - e, epochs)
        if e:
            block_copy(e, source).wait_recv()
            block_copy(e, epoch).wait_send()

        @pl.when(has_left)
        def _():
            edge_copy(e, 0, epoch).wait_send()
            edge_copy(e, 1, source).wait_recv()

        @pl.when(has_right)
        def _():
            edge_copy(e, 1, epoch).wait_send()
            edge_copy(e, 0, source).wait_recv()

    middle = jnp.zeros((cols - 2 * EDGE, own_rows), F32)
    for e in range(epochs):
        at = pl.ds(top + e * own_rows, own_rows)
        strip[at, :cols] = slots[e]
        strip[at, cols:] = jnp.transpose(jnp.concatenate([edges[0, e], middle, edges[1, e]], axis=0))
    convolve(strip[...], row_band_ref, col_band_ref, images_ref, mixed_ref)
    normal = gram(weight_ref, mixed_ref, total)
    side = 3 * GROUP
    normal = jnp.concatenate([normal, jnp.zeros((side, LANES - side), F32)], axis=1)
    mine[...] = normal

    def part_copy(t, source):
        return remote(mine, parts.at[source], part_send.at[t], part_recv.at[source],
                      epoch, lax.rem(tile + t, tiles))

    for t in range(1, tiles):
        part_copy(t, tile).start()
    for t in range(1, tiles):
        source = lax.rem(tile + tiles - t, tiles)
        part_copy(t, source).wait_recv()
        normal = normal + parts[source]
    for t in range(1, tiles):
        part_copy(t, tile).wait_send()
    coefs = solve(normal, count)
    apply(coefs, images_ref, science_ref, out_ref, total)


def local(template, science, row_profiles, col_profiles, coverage, stamp_rows, stamp_cols):
    count, taps = row_profiles.shape
    rows, cols = science.shape[1:]
    own_rows = template.shape[0]
    tiles, epochs = lax.axis_size("tile"), lax.axis_size("epoch")
    width = 2 * LANES
    top = -(-(taps // 2) // 8) * 8
    block = row_block(rows, taps - 1 + top - taps // 2, width)
    vmem = pl.BlockSpec(memory_space=pltpu.VMEM)
    dma = pltpu.SemaphoreType.DMA
    return pl.pallas_call(
        functools.partial(kernel, cols * tiles, top),
        out_shape=jax.ShapeDtypeStruct(science.shape, F32),
        in_specs=[vmem] * 7,
        out_specs=vmem,
        scratch_shapes=[
            pltpu.VMEM((epochs, own_rows, cols), F32),
            pltpu.VMEM((2, EDGE, own_rows), F32),
            pltpu.VMEM((2, epochs, EDGE, own_rows), F32),
            pltpu.VMEM((rows - block + width, width), F32),
            pltpu.VMEM((tiles, 3 * GROUP, LANES), F32),
            pltpu.VMEM((3 * GROUP, LANES), F32),
            pltpu.VMEM((count, rows, cols), F32),
            pltpu.VMEM((rows * GROUP, cols), F32),
            pltpu.VMEM((rows * GROUP, cols), F32),
            pltpu.VMEM((2, GROUP, width), F32),
            pltpu.VMEM((2, count, block, width), BF16),
            pltpu.VMEM((2, count, cols, width), BF16),
            dma((epochs,)),
            dma((epochs,)),
            dma((2, epochs)),
            dma((2, epochs)),
            dma((tiles,)),
            dma((tiles,)),
        ],
        compiler_params=pltpu.CompilerParams(
            collective_id=0, has_side_effects=True, vmem_limit_bytes=48 * 2**20
        ),
    )(
        template,
        science,
        row_profiles,
        col_profiles,
        coverage,
        stamp_rows.reshape(1, -1),
        stamp_cols.reshape(1, -1),
    )


def solution(mesh):
    in_specs = (
        P(("patch", "epoch"), "tile"),
        P(("patch", "epoch"), None, "tile"),
        P(),
        P(),
        P(("patch", "epoch"), "tile"),
        P(("patch", "tile")),
        P(("patch", "tile")),
    )
    out_specs = P(("patch", "epoch"), None, "tile")
    return jax.shard_map(local, mesh=mesh, in_specs=in_specs, out_specs=out_specs, check_vma=False)
```

```python
import functools

import jax
import jax.numpy as jnp
from jax import lax
from jax.experimental import pallas as pl
from jax.experimental.pallas import tpu as pltpu
from jax.sharding import PartitionSpec as P

S = 32
GROUP = 16
EDGE = 16
CHUNK = 16
UNROLL = 2
LANES = 128
ridge_weight = 1.0
F32 = jnp.float32
BF16 = jnp.bfloat16
NT = (((1,), (1,)), ((), ()))
NN = (((1,), (0,)), ((), ()))


def split(value):
    high = value.astype(BF16)
    return high, (value - high.astype(F32)).astype(BF16)


def toeplitz(profile_row, rows, shift, width):
    base = pltpu.roll(jnp.broadcast_to(profile_row, (8, width)), 0, 1, stride=1, stride_axis=0)
    turns = [(shift + first) % width for first in range(0, rows, 8)]
    return jnp.concatenate([pltpu.roll(base, turn, 1) if turn else base for turn in turns], axis=0)


def iota(shape, axis):
    return lax.broadcasted_iota(jnp.int32, shape, axis)


def row_block(rows, extra, width):
    best = 8
    for size in range(8, width - extra + 1, 8):
        if rows % size == 0:
            best = size
    return best


def xi_row(cols, total):
    start = lax.axis_index("tile") * cols
    return 2.0 * (start + iota((1, cols), 1)).astype(F32) / total - 1.0


def make_bands(rowp_ref, colp_ref, profile_ref, row_band_ref, col_band_ref, shift):
    count, taps = rowp_ref.shape
    width = profile_ref.shape[2]
    profile_ref[...] = jnp.zeros_like(profile_ref)
    profile_ref[0, :count, :taps] = rowp_ref[...]
    profile_ref[1, :count, :taps] = colp_ref[...]
    for b in range(count):
        band = split(toeplitz(profile_ref[0, b : b + 1, :], row_band_ref.shape[2], shift, width))
        row_band_ref[0, b], row_band_ref[1, b] = band
        band = split(toeplitz(profile_ref[1, b : b + 1, :], col_band_ref.shape[2], -(taps // 2), width))
        col_band_ref[0, b], col_band_ref[1, b] = band


def column_pass(strip, at, col_band_ref, across_ref):
    count, _, lanes = across_ref.shape
    cols = lanes // 2
    high, low = split(strip)
    dot = functools.partial(lax.dot_general, dimension_numbers=NT, preferred_element_type=F32)
    for pair in range(0, count, 2):
        members = [b for b in (pair, pair + 1) if b < count]
        small = dot(low, jnp.concatenate([col_band_ref[0, b] for b in members], axis=0))
        for k, b in enumerate(members):
            big = dot(high, jnp.concatenate([col_band_ref[0, b], col_band_ref[1, b]], axis=0))
            across = big[:, :cols] + (big[:, cols:] + small[:, k * cols : (k + 1) * cols])
            across_ref[b, at, :] = jnp.concatenate(split(across), axis=1)


def row_pass(row_band_ref, across_ref, images_ref, mixed_ref):
    count, rows, cols = images_ref.shape
    block, width = row_band_ref.shape[2:]
    dot = functools.partial(lax.dot_general, dimension_numbers=NN, preferred_element_type=F32)
    for b in range(count):
        for start in range(0, rows, block):
            across = across_ref[b, start : start + width, :]
            big = dot(row_band_ref[0, b], across)
            small = dot(row_band_ref[1, b], across[:, :cols])
            piece = big[:, :cols] + (big[:, cols:] + small)
            images_ref[b, start : start + block, :] = piece
            mixed_ref[pl.ds(start * GROUP + b, block, stride=GROUP), :] = piece


def make_weight(srow_ref, scol_ref, cov_ref, weight_ref):
    cols = weight_ref.shape[1]
    stamps = srow_ref.shape[1]
    at = iota((cols, stamps), 0) - scol_ref[...]
    cols_in = jnp.where((at >= 0) & (at < S), cov_ref[...].astype(F32), 0.0).astype(BF16)
    size = CHUNK * GROUP

    def body(chunk, carry):
        at_row = chunk * CHUNK + iota((size, 1), 0) // GROUP - srow_ref[...]
        rows_in = jnp.where((at_row >= 0) & (at_row < S), 1.0, 0.0).astype(BF16)
        at = pl.ds(pl.multiple_of(chunk * size, size), size)
        weight_ref[at, :] = lax.dot_general(rows_in, cols_in, NT, preferred_element_type=F32)
        return carry

    lax.fori_loop(0, weight_ref.shape[0] // size, body, 0)


def gram(weight_ref, mixed_ref, total):
    height, cols = mixed_ref.shape
    rows = height // GROUP
    xi = xi_row(cols, total)
    size = CHUNK * GROUP

    def lay(values):
        return jnp.concatenate(
            [
                jnp.concatenate([v[k * GROUP : (k + 1) * GROUP] for k in range(CHUNK)], axis=1)
                for v in values
            ],
            axis=0,
        )

    def body(chunk, acc):
        at = pl.ds(pl.multiple_of(chunk * size, size), size)
        base = mixed_ref[at, :]
        weight = weight_ref[at, :]
        y = chunk * CHUNK + iota((size, 1), 0) // GROUP
        eta = 2.0 * y.astype(F32) / rows - 1.0
        feats = (base, base * xi, base * eta)
        right = jnp.concatenate(split(lay(feats)), axis=0)
        left = jnp.concatenate(split(lay([f * weight for f in feats])), axis=0)
        return acc + lax.dot_general(left, right, NT, preferred_element_type=F32)

    side = 3 * GROUP
    sums = lax.fori_loop(0, rows // CHUNK, body, jnp.zeros((2 * side, 2 * side), F32), unroll=UNROLL)
    return sums[:side, :side] + (sums[:side, side:] + sums[side:, :side] + sums[side:, side:])


def solve(normal, count):
    side = 3 * GROUP
    row, col = iota((side, LANES), 0), iota((side, LANES), 1)

    def used(k):
        return ((k % GROUP < count) & (k < side)) | (k == count)

    rhs = normal[:, count + 1 : count + 2]
    system = jnp.where(used(row) & used(col), normal, 0.0) + ridge_weight * jnp.where(row == col, 1.0, 0.0)
    system = jnp.where((col == side) & used(row), rhs, system)
    unknowns = [k for k in range(side) if (k % GROUP < count) or k == count]
    for p in unknowns:
        pivot_row = system[p : p + 1, :]
        factor = system[:, p : p + 1] / system[p : p + 1, p : p + 1]
        factor = jnp.where(row[:, :1] == p, 0.0, factor)
        system = system - factor * pivot_row
    diagonal = jnp.sum(jnp.where(row == col, system, 0.0), axis=1, keepdims=True)
    return system[:, side : side + 1] / diagonal


def apply(coefs, images_ref, science_ref, out_ref, total):
    count, rows, cols = images_ref.shape
    xi = xi_row(cols, total)
    eta = 2.0 * iota((rows, 1), 0).astype(F32) / rows - 1.0
    field = jnp.broadcast_to(coefs[count : count + 1, :], (rows, cols))
    for b in range(count):
        flat = coefs[b : b + 1] + coefs[GROUP + b : GROUP + b + 1] * xi
        field = field + images_ref[b] * (flat + coefs[2 * GROUP + b : 2 * GROUP + b + 1] * eta)
    out_ref[0] = science_ref[0] - field


def fill_rest(mixed_ref, science, count):
    rows = science.shape[0]
    mixed_ref[pl.ds(count, rows, stride=GROUP), :] = jnp.ones_like(science)
    mixed_ref[pl.ds(count + 1, rows, stride=GROUP), :] = science
    for spare in range(count + 2, GROUP):
        mixed_ref[pl.ds(spare, rows, stride=GROUP), :] = jnp.zeros_like(science)


def remote(source, target, send, recv, epoch, tile):
    return pltpu.make_async_remote_copy(
        src_ref=source,
        dst_ref=target,
        send_sem=send,
        recv_sem=recv,
        device_id={"epoch": epoch, "tile": tile},
        device_id_type=pl.DeviceIdType.MESH,
    )


def kernel(total, top, template_in, science_in, rowp_in, colp_in, cov_in, srow_in, scol_in, out_ref,
           science_ref, rowp_ref, colp_ref, cov_ref, srow_ref, scol_ref,
           slots, pack, edges, across_ref, parts, mine, images_ref, mixed_ref, weight_ref, profile_ref,
           row_band_ref, col_band_ref, slot_send, slot_recv, edge_send, edge_recv, part_send, part_recv, load_sem):
    count, rows, cols = images_ref.shape
    taps = rowp_ref.shape[1]
    epochs, own_rows, _ = slots.shape
    tiles = parts.shape[0]
    epoch, tile = lax.axis_index("epoch"), lax.axis_index("tile")

    loads = [
        pltpu.make_async_copy(source, target, load_sem.at[k])
        for k, (source, target) in enumerate(
            [
                (template_in, slots.at[epoch]),
                (cov_in, cov_ref),
                (srow_in, srow_ref),
                (scol_in, scol_ref),
                (rowp_in, rowp_ref),
                (colp_in, colp_ref),
                (science_in, science_ref),
            ]
        )
    ]
    for load in loads:
        load.start()
    barrier = pltpu.get_barrier_semaphore()
    for e in range(epochs):
        for t in range(tiles):
            if e or t:
                where = {"epoch": lax.rem(epoch + e, epochs), "tile": lax.rem(tile + t, tiles)}
                pl.semaphore_signal(barrier, inc=1, device_id=where, device_id_type=pl.DeviceIdType.MESH)
    loads[0].wait()
    flipped = jnp.transpose(slots[epoch])
    pack[0] = flipped[:EDGE]
    pack[1] = flipped[cols - EDGE :]
    for load in loads[1:4]:
        load.wait()
    make_weight(srow_ref, scol_ref, cov_ref, weight_ref)
    pl.semaphore_wait(barrier, epochs * tiles - 1)

    def block_copy(e, source):
        return remote(slots.at[epoch], slots.at[source], slot_send.at[e], slot_recv.at[source],
                      lax.rem(epoch + e, epochs), tile)

    def edge_copy(e, side, source):
        beside = tile - 1 if side == 0 else tile + 1
        return remote(pack.at[side], edges.at[side, source], edge_send.at[side, e], edge_recv.at[side, source],
                      lax.rem(epoch + e, epochs), beside)

    has_left, has_right = tile > 0, tile < tiles - 1
    order = sorted(range(epochs), key=lambda e: -e * (epochs - e))
    for e in order:
        if e:
            block_copy(e, epoch).start()

        @pl.when(has_left)
        def _():
            edge_copy(e, 0, epoch).start()

        @pl.when(has_right)
        def _():
            edge_copy(e, 1, epoch).start()

    for load in loads[4:]:
        load.wait()
    make_bands(rowp_ref, colp_ref, profile_ref, row_band_ref, col_band_ref, top - taps // 2)
    fill_rest(mixed_ref, science_ref[0], count)
    high = across_ref.shape[1]
    across_ref[:, :top, :] = jnp.zeros((count, top, 2 * cols), BF16)
    across_ref[:, top + rows :, :] = jnp.zeros((count, high - top - rows, 2 * cols), BF16)

    @pl.when(tile == tiles - 1)
    def _():
        edges[0] = jnp.zeros(edges.shape[1:], F32)

    @pl.when(tile == 0)
    def _():
        edges[1] = jnp.zeros(edges.shape[1:], F32)

    def arrive(source):
        e = lax.rem(epoch + epochs - source, epochs)

        @pl.when(e != 0)
        def _():
            block_copy(e, source).wait_recv()

        @pl.when(has_left)
        def _():
            edge_copy(e, 1, source).wait_recv()

        @pl.when(has_right)
        def _():
            edge_copy(e, 0, source).wait_recv()

    middle = jnp.zeros((cols - 2 * EDGE, own_rows), F32)

    def strip_of(source):
        beside = jnp.transpose(jnp.concatenate([edges[0, source], middle, edges[1, source]], axis=0))
        return jnp.concatenate([slots[source], beside], axis=1)

    groups = 2 if epochs % 2 == 0 and own_rows % 16 == 0 else 1
    each = epochs // groups
    for turn in range(groups):
        group = lax.rem(epoch // each + turn, groups)
        for k in range(each):
            arrive(group * each + k)
        strip = jnp.concatenate([strip_of(group * each + k) for k in range(each)], axis=0)
        height = each * own_rows
        at = pl.ds(pl.multiple_of(top + group * height, 16), height) if groups > 1 else pl.ds(top, height)
        column_pass(strip, at, col_band_ref, across_ref)
    row_pass(row_band_ref, across_ref, images_ref, mixed_ref)
    normal = gram(weight_ref, mixed_ref, total)
    side = 3 * GROUP
    normal = jnp.concatenate([normal, jnp.zeros((side, LANES - side), F32)], axis=1)
    mine[...] = normal

    def part_copy(t, source):
        return remote(mine, parts.at[source], part_send.at[t], part_recv.at[source],
                      epoch, lax.rem(tile + t, tiles))

    for t in range(1, tiles):
        part_copy(t, tile).start()
    for t in range(1, tiles):
        source = lax.rem(tile + tiles - t, tiles)
        part_copy(t, source).wait_recv()
        normal = normal + parts[source]
    for t in range(1, tiles):
        part_copy(t, tile).wait_send()
    for e in range(epochs):
        if e:
            block_copy(e, epoch).wait_send()

        @pl.when(has_left)
        def _():
            edge_copy(e, 0, epoch).wait_send()

        @pl.when(has_right)
        def _():
            edge_copy(e, 1, epoch).wait_send()

    coefs = solve(normal, count)
    apply(coefs, images_ref, science_ref, out_ref, total)


def local(template, science, row_profiles, col_profiles, coverage, stamp_rows, stamp_cols):
    count, taps = row_profiles.shape
    rows, cols = science.shape[1:]
    own_rows = template.shape[0]
    tiles, epochs = lax.axis_size("tile"), lax.axis_size("epoch")
    width = 2 * LANES
    top = -(-(taps // 2) // 16) * 16
    block = row_block(rows, taps - 1 + top - taps // 2, width)
    vmem = pl.BlockSpec(memory_space=pltpu.VMEM)
    dma = pltpu.SemaphoreType.DMA
    return pl.pallas_call(
        functools.partial(kernel, cols * tiles, top),
        out_shape=jax.ShapeDtypeStruct(science.shape, F32),
        in_specs=[pl.BlockSpec(memory_space=pl.ANY)] * 7,
        out_specs=vmem,
        scratch_shapes=[
            pltpu.VMEM(science.shape, F32),
            pltpu.VMEM(row_profiles.shape, F32),
            pltpu.VMEM(col_profiles.shape, F32),
            pltpu.VMEM(coverage.shape, jnp.int32),
            pltpu.VMEM((1, stamp_rows.shape[0]), jnp.int32),
            pltpu.VMEM((1, stamp_cols.shape[0]), jnp.int32),
            pltpu.VMEM((epochs, own_rows, cols), F32),
            pltpu.VMEM((2, EDGE, own_rows), F32),
            pltpu.VMEM((2, epochs, EDGE, own_rows), F32),
            pltpu.VMEM((count, rows - block + width, 2 * cols), BF16),
            pltpu.VMEM((tiles, 3 * GROUP, LANES), F32),
            pltpu.VMEM((3 * GROUP, LANES), F32),
            pltpu.VMEM((count, rows, cols), F32),
            pltpu.VMEM((rows * GROUP, cols), F32),
            pltpu.VMEM((rows * GROUP, cols), F32),
            pltpu.VMEM((2, GROUP, width), F32),
            pltpu.VMEM((2, count, block, width), BF16),
            pltpu.VMEM((2, count, cols, width), BF16),
            dma((epochs,)),
            dma((epochs,)),
            dma((2, epochs)),
            dma((2, epochs)),
            dma((tiles,)),
            dma((tiles,)),
            dma((7,)),
        ],
        compiler_params=pltpu.CompilerParams(
            collective_id=0, has_side_effects=True, vmem_limit_bytes=63 * 2**20
        ),
    )(
        template,
        science,
        row_profiles,
        col_profiles,
        coverage,
        stamp_rows.reshape(1, -1),
        stamp_cols.reshape(1, -1),
    )


def solution(mesh):
    in_specs = (
        P(("patch", "epoch"), "tile"),
        P(("patch", "epoch"), None, "tile"),
        P(),
        P(),
        P(("patch", "epoch"), "tile"),
        P(("patch", "tile")),
        P(("patch", "tile")),
    )
    out_specs = P(("patch", "epoch"), None, "tile")
    return jax.shard_map(local, mesh=mesh, in_specs=in_specs, out_specs=out_specs, check_vma=False)
```

```python
import functools

import jax
import jax.numpy as jnp
from jax import lax
from jax.experimental import pallas as pl
from jax.experimental.pallas import tpu as pltpu
from jax.sharding import PartitionSpec as P

S = 32
GROUP = 16
EDGE = 16
CHUNK = 64
LANES = 128
ridge_weight = 1.0
F32 = jnp.float32
BF16 = jnp.bfloat16
NT = (((1,), (1,)), ((), ()))
NN = (((1,), (0,)), ((), ()))


def split(value):
    high = value.astype(BF16)
    return high, (value - high.astype(F32)).astype(BF16)


def toeplitz(profile_row, rows, shift, width):
    base = pltpu.roll(jnp.broadcast_to(profile_row, (8, width)), 0, 1, stride=1, stride_axis=0)
    turns = [(shift + first) % width for first in range(0, rows, 8)]
    return jnp.concatenate([pltpu.roll(base, turn, 1) if turn else base for turn in turns], axis=0)


def iota(shape, axis):
    return lax.broadcasted_iota(jnp.int32, shape, axis)


def row_block(rows, extra, width):
    best = 8
    for size in range(8, width - extra + 1, 8):
        if rows % size == 0:
            best = size
    return best


def xi_row(cols, total):
    start = lax.axis_index("tile") * cols
    return 2.0 * (start + iota((1, cols), 1)).astype(F32) / total - 1.0


def make_bands(rowp_ref, colp_ref, profile_ref, row_band_ref, col_band_ref, shift):
    count, taps = rowp_ref.shape
    width = profile_ref.shape[2]
    profile_ref[...] = jnp.zeros_like(profile_ref)
    profile_ref[0, :count, :taps] = rowp_ref[...]
    profile_ref[1, :count, :taps] = colp_ref[...]
    for b in range(count):
        band = split(toeplitz(profile_ref[0, b : b + 1, :], row_band_ref.shape[2], shift, width))
        row_band_ref[0, b], row_band_ref[1, b] = band
        band = split(toeplitz(profile_ref[1, b : b + 1, :], col_band_ref.shape[2], -(taps // 2), width))
        col_band_ref[0, b], col_band_ref[1, b] = band


def column_pass(strip, at, col_band_ref, across_ref):
    count, _, lanes = across_ref.shape
    cols = lanes // 2
    high, low = split(strip)
    dot = functools.partial(lax.dot_general, dimension_numbers=NT, preferred_element_type=F32)
    for pair in range(0, count, 2):
        members = [b for b in (pair, pair + 1) if b < count]
        small = dot(low, jnp.concatenate([col_band_ref[0, b] for b in members], axis=0))
        for k, b in enumerate(members):
            big = dot(high, jnp.concatenate([col_band_ref[0, b], col_band_ref[1, b]], axis=0))
            across = big[:, :cols] + (big[:, cols:] + small[:, k * cols : (k + 1) * cols])
            across_ref[b, at, :] = jnp.concatenate(split(across), axis=1)


def row_pass(row_band_ref, across_ref, images_ref, mixed_ref):
    count, rows, cols = images_ref.shape
    block, width = row_band_ref.shape[2:]
    dot = functools.partial(lax.dot_general, dimension_numbers=NN, preferred_element_type=F32)
    for b in range(count):
        for start in range(0, rows, block):
            across = across_ref[b, start : start + width, :]
            big = dot(row_band_ref[0, b], across)
            small = dot(row_band_ref[1, b], across[:, :cols])
            piece = big[:, :cols] + (big[:, cols:] + small)
            images_ref[b, start : start + block, :] = piece
            mixed_ref[pl.ds(start * GROUP + b, block, stride=GROUP), :] = piece


def chunk_rows(rows):
    return max(size for size in range(1, CHUNK + 1) if rows % size == 0)


def make_weight(srow_ref, scol_ref, cov_ref, weight_ref):
    cols = weight_ref.shape[1]
    stamps = srow_ref.shape[1]
    at = iota((cols, stamps), 0) - scol_ref[...]
    cols_in = jnp.where((at >= 0) & (at < S), cov_ref[...].astype(F32), 0.0).astype(BF16)
    step = chunk_rows(weight_ref.shape[0] // GROUP)
    size = step * GROUP

    def body(chunk, carry):
        at_row = chunk * step + iota((size, 1), 0) // GROUP - srow_ref[...]
        rows_in = jnp.where((at_row >= 0) & (at_row < S), 1.0, 0.0).astype(BF16)
        at = pl.ds(pl.multiple_of(chunk * size, size), size)
        weight_ref[at, :] = lax.dot_general(rows_in, cols_in, NT, preferred_element_type=F32)
        return carry

    lax.fori_loop(0, weight_ref.shape[0] // size, body, 0)


def gram(weight_ref, mixed_ref, total):
    height, cols = mixed_ref.shape
    rows = height // GROUP
    xi = xi_row(cols, total)
    step = chunk_rows(rows)
    size = step * GROUP

    def lay(values):
        return jnp.concatenate(
            [
                jnp.concatenate([v[k * GROUP : (k + 1) * GROUP] for k in range(step)], axis=1)
                for v in values
            ],
            axis=0,
        )

    def body(chunk, acc):
        at = pl.ds(pl.multiple_of(chunk * size, size), size)
        base = mixed_ref[at, :]
        weight = weight_ref[at, :]
        y = chunk * step + iota((size, 1), 0) // GROUP
        eta = 2.0 * y.astype(F32) / rows - 1.0
        feats = (base, base * xi, base * eta)
        right = jnp.concatenate(split(lay(feats)), axis=0)
        left = jnp.concatenate(split(lay([f * weight for f in feats])), axis=0)
        return acc + lax.dot_general(left, right, NT, preferred_element_type=F32)

    side = 3 * GROUP
    sums = lax.fori_loop(0, rows // step, body, jnp.zeros((2 * side, 2 * side), F32))
    return sums[:side, :side] + (sums[:side, side:] + sums[side:, :side] + sums[side:, side:])


def solve(normal, count):
    side = 3 * GROUP
    row, col = iota((side, LANES), 0), iota((side, LANES), 1)

    def used(k):
        return ((k % GROUP < count) & (k < side)) | (k == count)

    rhs = normal[:, count + 1 : count + 2]
    system = jnp.where(used(row) & used(col), normal, 0.0) + ridge_weight * jnp.where(row == col, 1.0, 0.0)
    system = jnp.where((col == side) & used(row), rhs, system)
    unknowns = [k for k in range(side) if (k % GROUP < count) or k == count]
    for p in unknowns:
        pivot_row = system[p : p + 1, :]
        factor = system[:, p : p + 1] / system[p : p + 1, p : p + 1]
        factor = jnp.where(row[:, :1] == p, 0.0, factor)
        system = system - factor * pivot_row
    diagonal = jnp.sum(jnp.where(row == col, system, 0.0), axis=1, keepdims=True)
    return system[:, side : side + 1] / diagonal


def apply(coefs, images_ref, science_ref, out_ref, total):
    count, rows, cols = images_ref.shape
    xi = xi_row(cols, total)
    eta = 2.0 * iota((rows, 1), 0).astype(F32) / rows - 1.0
    field = jnp.broadcast_to(coefs[count : count + 1, :], (rows, cols))
    for b in range(count):
        flat = coefs[b : b + 1] + coefs[GROUP + b : GROUP + b + 1] * xi
        field = field + images_ref[b] * (flat + coefs[2 * GROUP + b : 2 * GROUP + b + 1] * eta)
    out_ref[0] = science_ref[0] - field


def fill_rest(mixed_ref, science, count):
    rows = science.shape[0]
    mixed_ref[pl.ds(count, rows, stride=GROUP), :] = jnp.ones_like(science)
    mixed_ref[pl.ds(count + 1, rows, stride=GROUP), :] = science
    for spare in range(count + 2, GROUP):
        mixed_ref[pl.ds(spare, rows, stride=GROUP), :] = jnp.zeros_like(science)


def remote(source, target, send, recv, epoch, tile):
    return pltpu.make_async_remote_copy(
        src_ref=source,
        dst_ref=target,
        send_sem=send,
        recv_sem=recv,
        device_id={"epoch": epoch, "tile": tile},
        device_id_type=pl.DeviceIdType.MESH,
    )


def kernel(total, top, template_in, science_in, rowp_in, colp_in, cov_in, srow_in, scol_in, out_ref,
           science_ref, rowp_ref, colp_ref, cov_ref, srow_ref, scol_ref,
           slots, pack, edges, across_ref, parts, mine, images_ref, mixed_ref, weight_ref, profile_ref,
           row_band_ref, col_band_ref, slot_send, slot_recv, edge_send, edge_recv, part_send, part_recv, load_sem):
    count, rows, cols = images_ref.shape
    taps = rowp_ref.shape[1]
    epochs, own_rows, _ = slots.shape
    tiles = parts.shape[0]
    epoch, tile = lax.axis_index("epoch"), lax.axis_index("tile")

    loads = [
        pltpu.make_async_copy(source, target, load_sem.at[k])
        for k, (source, target) in enumerate(
            [
                (template_in, slots.at[epoch]),
                (cov_in, cov_ref),
                (srow_in, srow_ref),
                (scol_in, scol_ref),
                (rowp_in, rowp_ref),
                (colp_in, colp_ref),
                (science_in, science_ref),
            ]
        )
    ]
    for load in loads:
        load.start()
    barrier = pltpu.get_barrier_semaphore()
    for e in range(epochs):
        for t in range(tiles):
            if e or t:
                where = {"epoch": lax.rem(epoch + e, epochs), "tile": lax.rem(tile + t, tiles)}
                pl.semaphore_signal(barrier, inc=1, device_id=where, device_id_type=pl.DeviceIdType.MESH)
    loads[0].wait()
    flipped = jnp.transpose(slots[epoch])
    pack[0] = flipped[:EDGE]
    pack[1] = flipped[cols - EDGE :]
    pl.semaphore_wait(barrier, epochs * tiles - 1)

    def block_copy(e, source):
        return remote(slots.at[epoch], slots.at[source], slot_send.at[e], slot_recv.at[source],
                      lax.rem(epoch + e, epochs), tile)

    def edge_copy(e, side, source):
        beside = tile - 1 if side == 0 else tile + 1
        return remote(pack.at[side], edges.at[side, source], edge_send.at[side, e], edge_recv.at[side, source],
                      lax.rem(epoch + e, epochs), beside)

    has_left, has_right = tile > 0, tile < tiles - 1
    order = sorted(range(epochs), key=lambda e: -e * (epochs - e))
    for e in order:
        if e:
            block_copy(e, epoch).start()

        @pl.when(has_left)
        def _():
            edge_copy(e, 0, epoch).start()

        @pl.when(has_right)
        def _():
            edge_copy(e, 1, epoch).start()

    for load in loads[1:]:
        load.wait()
    make_weight(srow_ref, scol_ref, cov_ref, weight_ref)
    make_bands(rowp_ref, colp_ref, profile_ref, row_band_ref, col_band_ref, top - taps // 2)
    fill_rest(mixed_ref, science_ref[0], count)
    high = across_ref.shape[1]
    across_ref[:, :top, :] = jnp.zeros((count, top, 2 * cols), BF16)
    across_ref[:, top + rows :, :] = jnp.zeros((count, high - top - rows, 2 * cols), BF16)

    @pl.when(tile == tiles - 1)
    def _():
        edges[0] = jnp.zeros(edges.shape[1:], F32)

    @pl.when(tile == 0)
    def _():
        edges[1] = jnp.zeros(edges.shape[1:], F32)

    def arrive(source):
        e = lax.rem(epoch + epochs - source, epochs)

        @pl.when(e != 0)
        def _():
            block_copy(e, source).wait_recv()

        @pl.when(has_left)
        def _():
            edge_copy(e, 1, source).wait_recv()

        @pl.when(has_right)
        def _():
            edge_copy(e, 0, source).wait_recv()

    middle = jnp.zeros((cols - 2 * EDGE, own_rows), F32)

    def strip_of(source):
        beside = jnp.transpose(jnp.concatenate([edges[0, source], middle, edges[1, source]], axis=0))
        return jnp.concatenate([slots[source], beside], axis=1)

    groups = 2 if epochs % 2 == 0 and own_rows % 16 == 0 else 1
    each = epochs // groups
    for turn in range(groups):
        group = lax.rem(epoch // each + turn, groups)
        for k in range(each):
            arrive(group * each + k)
        strip = jnp.concatenate([strip_of(group * each + k) for k in range(each)], axis=0)
        height = each * own_rows
        at = pl.ds(pl.multiple_of(top + group * height, 16), height) if groups > 1 else pl.ds(top, height)
        column_pass(strip, at, col_band_ref, across_ref)
    row_pass(row_band_ref, across_ref, images_ref, mixed_ref)
    normal = gram(weight_ref, mixed_ref, total)
    side = 3 * GROUP
    normal = jnp.concatenate([normal, jnp.zeros((side, LANES - side), F32)], axis=1)
    mine[...] = normal

    def part_copy(t, source):
        return remote(mine, parts.at[source], part_send.at[t], part_recv.at[source],
                      epoch, lax.rem(tile + t, tiles))

    for t in range(1, tiles):
        part_copy(t, tile).start()
    for t in range(1, tiles):
        source = lax.rem(tile + tiles - t, tiles)
        part_copy(t, source).wait_recv()
        normal = normal + parts[source]
    for t in range(1, tiles):
        part_copy(t, tile).wait_send()
    for e in range(epochs):
        if e:
            block_copy(e, epoch).wait_send()

        @pl.when(has_left)
        def _():
            edge_copy(e, 0, epoch).wait_send()

        @pl.when(has_right)
        def _():
            edge_copy(e, 1, epoch).wait_send()

    coefs = solve(normal, count)
    apply(coefs, images_ref, science_ref, out_ref, total)


def local(template, science, row_profiles, col_profiles, coverage, stamp_rows, stamp_cols):
    count, taps = row_profiles.shape
    rows, cols = science.shape[1:]
    own_rows = template.shape[0]
    tiles, epochs = lax.axis_size("tile"), lax.axis_size("epoch")
    width = 2 * LANES
    top = -(-(taps // 2) // 16) * 16
    block = row_block(rows, taps - 1 + top - taps // 2, width)
    vmem = pl.BlockSpec(memory_space=pltpu.VMEM)
    dma = pltpu.SemaphoreType.DMA
    return pl.pallas_call(
        functools.partial(kernel, cols * tiles, top),
        out_shape=jax.ShapeDtypeStruct(science.shape, F32),
        in_specs=[pl.BlockSpec(memory_space=pl.ANY)] * 7,
        out_specs=vmem,
        scratch_shapes=[
            pltpu.VMEM(science.shape, F32),
            pltpu.VMEM(row_profiles.shape, F32),
            pltpu.VMEM(col_profiles.shape, F32),
            pltpu.VMEM(coverage.shape, jnp.int32),
            pltpu.VMEM((1, stamp_rows.shape[0]), jnp.int32),
            pltpu.VMEM((1, stamp_cols.shape[0]), jnp.int32),
            pltpu.VMEM((epochs, own_rows, cols), F32),
            pltpu.VMEM((2, EDGE, own_rows), F32),
            pltpu.VMEM((2, epochs, EDGE, own_rows), F32),
            pltpu.VMEM((count, rows - block + width, 2 * cols), BF16),
            pltpu.VMEM((tiles, 3 * GROUP, LANES), F32),
            pltpu.VMEM((3 * GROUP, LANES), F32),
            pltpu.VMEM((count, rows, cols), F32),
            pltpu.VMEM((rows * GROUP, cols), F32),
            pltpu.VMEM((rows * GROUP, cols), F32),
            pltpu.VMEM((2, GROUP, width), F32),
            pltpu.VMEM((2, count, block, width), BF16),
            pltpu.VMEM((2, count, cols, width), BF16),
            dma((epochs,)),
            dma((epochs,)),
            dma((2, epochs)),
            dma((2, epochs)),
            dma((tiles,)),
            dma((tiles,)),
            dma((7,)),
        ],
        compiler_params=pltpu.CompilerParams(
            collective_id=0, has_side_effects=True, vmem_limit_bytes=63 * 2**20
        ),
    )(
        template,
        science,
        row_profiles,
        col_profiles,
        coverage,
        stamp_rows.reshape(1, -1),
        stamp_cols.reshape(1, -1),
    )


def solution(mesh):
    in_specs = (
        P(("patch", "epoch"), "tile"),
        P(("patch", "epoch"), None, "tile"),
        P(),
        P(),
        P(("patch", "epoch"), "tile"),
        P(("patch", "tile")),
        P(("patch", "tile")),
    )
    out_specs = P(("patch", "epoch"), None, "tile")
    return jax.shard_map(local, mesh=mesh, in_specs=in_specs, out_specs=out_specs, check_vma=False)
```

```python
import functools

import jax
import jax.numpy as jnp
from jax import lax
from jax.experimental import pallas as pl
from jax.experimental.pallas import tpu as pltpu
from jax.sharding import PartitionSpec as P

S = 32
GROUP = 16
EDGE = 16
CHUNK = 64
LANES = 128
ridge_weight = 1.0
F32 = jnp.float32
BF16 = jnp.bfloat16
NT = (((1,), (1,)), ((), ()))
NN = (((1,), (0,)), ((), ()))


def split(value):
    high = value.astype(BF16)
    return high, (value - high.astype(F32)).astype(BF16)


def toeplitz(profile_row, rows, shift, width):
    base = pltpu.roll(jnp.broadcast_to(profile_row, (8, width)), 0, 1, stride=1, stride_axis=0)
    turns = [(shift + first) % width for first in range(0, rows, 8)]
    return jnp.concatenate([pltpu.roll(base, turn, 1) if turn else base for turn in turns], axis=0)


def iota(shape, axis):
    return lax.broadcasted_iota(jnp.int32, shape, axis)


def row_block(rows, extra, width):
    best = 8
    for size in range(8, width - extra + 1, 8):
        if rows % size == 0:
            best = size
    return best


def xi_row(cols, total):
    start = lax.axis_index("tile") * cols
    return 2.0 * (start + iota((1, cols), 1)).astype(F32) / total - 1.0


def make_bands(rowp_ref, colp_ref, profile_ref, row_band_ref, col_band_ref, shift):
    count, taps = rowp_ref.shape
    width = profile_ref.shape[2]
    profile_ref[...] = jnp.zeros_like(profile_ref)
    profile_ref[0, :count, :taps] = rowp_ref[...]
    profile_ref[1, :count, :taps] = colp_ref[...]
    for b in range(count):
        band = split(toeplitz(profile_ref[0, b : b + 1, :], row_band_ref.shape[2], shift, width))
        row_band_ref[0, b], row_band_ref[1, b] = band
        band = split(toeplitz(profile_ref[1, b : b + 1, :], col_band_ref.shape[2], -(taps // 2), width))
        col_band_ref[0, b], col_band_ref[1, b] = band


def column_pass(strip, at, col_band_ref, across_ref):
    count, _, lanes = across_ref.shape
    cols = lanes // 2
    high, low = split(strip)
    dot = functools.partial(lax.dot_general, dimension_numbers=NT, preferred_element_type=F32)
    for pair in range(0, count, 2):
        members = [b for b in (pair, pair + 1) if b < count]
        small = dot(low, jnp.concatenate([col_band_ref[0, b] for b in members], axis=0))
        for k, b in enumerate(members):
            big = dot(high, jnp.concatenate([col_band_ref[0, b], col_band_ref[1, b]], axis=0))
            across = big[:, :cols] + (big[:, cols:] + small[:, k * cols : (k + 1) * cols])
            across_ref[b, at, :] = jnp.concatenate(split(across), axis=1)


def row_pass(row_band_ref, across_ref, images_ref, mixed_ref):
    count, rows, cols = images_ref.shape
    block, width = row_band_ref.shape[2:]
    dot = functools.partial(lax.dot_general, dimension_numbers=NN, preferred_element_type=F32)
    for b in range(count):
        for start in range(0, rows, block):
            across = across_ref[b, start : start + width, :]
            big = dot(row_band_ref[0, b], across)
            small = dot(row_band_ref[1, b], across[:, :cols])
            piece = big[:, :cols] + (big[:, cols:] + small)
            images_ref[b, start : start + block, :] = piece
            mixed_ref[pl.ds(start * GROUP + b, block, stride=GROUP), :] = piece


def chunk_rows(rows):
    return max(size for size in range(1, CHUNK + 1) if rows % size == 0)


def make_weight(srow_ref, scol_ref, cov_ref, weight_ref):
    cols = weight_ref.shape[1]
    stamps = srow_ref.shape[1]
    at = iota((cols, stamps), 0) - scol_ref[...]
    cols_in = jnp.where((at >= 0) & (at < S), cov_ref[...].astype(F32), 0.0).astype(BF16)
    step = chunk_rows(weight_ref.shape[0] // GROUP)
    size = step * GROUP

    def body(chunk, carry):
        at_row = chunk * step + iota((size, 1), 0) // GROUP - srow_ref[...]
        rows_in = jnp.where((at_row >= 0) & (at_row < S), 1.0, 0.0).astype(BF16)
        at = pl.ds(pl.multiple_of(chunk * size, size), size)
        weight_ref[at, :] = lax.dot_general(rows_in, cols_in, NT, preferred_element_type=F32)
        return carry

    lax.fori_loop(0, weight_ref.shape[0] // size, body, 0)


def gram(weight_ref, mixed_ref, total):
    height, cols = mixed_ref.shape
    rows = height // GROUP
    xi = xi_row(cols, total)
    step = chunk_rows(rows)
    size = step * GROUP

    def lay(values):
        return jnp.concatenate(
            [
                jnp.concatenate([v[k * GROUP : (k + 1) * GROUP] for k in range(step)], axis=1)
                for v in values
            ],
            axis=0,
        )

    def body(chunk, acc):
        at = pl.ds(pl.multiple_of(chunk * size, size), size)
        base = mixed_ref[at, :]
        weight = weight_ref[at, :]
        y = chunk * step + iota((size, 1), 0) // GROUP
        eta = 2.0 * y.astype(F32) / rows - 1.0
        feats = (base, base * xi, base * eta)
        right = jnp.concatenate(split(lay(feats)), axis=0)
        left = jnp.concatenate(split(lay([f * weight for f in feats])), axis=0)
        return acc + lax.dot_general(left, right, NT, preferred_element_type=F32)

    side = 3 * GROUP
    sums = lax.fori_loop(0, rows // step, body, jnp.zeros((2 * side, 2 * side), F32))
    return sums[:side, :side] + (sums[:side, side:] + sums[side:, :side] + sums[side:, side:])


def solve(normal, count):
    side = 3 * GROUP
    row, col = iota((side, LANES), 0), iota((side, LANES), 1)

    def used(k):
        return ((k % GROUP < count) & (k < side)) | (k == count)

    rhs = normal[:, count + 1 : count + 2]
    system = jnp.where(used(row) & used(col), normal, 0.0) + ridge_weight * jnp.where(row == col, 1.0, 0.0)
    system = jnp.where((col == side) & used(row), rhs, system)
    unknowns = [k for k in range(side) if (k % GROUP < count) or k == count]
    for p in unknowns:
        pivot_row = system[p : p + 1, :]
        scaled = pivot_row / system[p : p + 1, p : p + 1]
        factor = jnp.where(row[:, :1] == p, 0.0, system[:, p : p + 1])
        system = system - factor * scaled
    diagonal = jnp.sum(jnp.where(row == col, system, 0.0), axis=1, keepdims=True)
    return system[:, side : side + 1] / diagonal


def apply(coefs, images_ref, science_ref, out_ref, total):
    count, rows, cols = images_ref.shape
    xi = xi_row(cols, total)
    eta = 2.0 * iota((rows, 1), 0).astype(F32) / rows - 1.0
    field = jnp.broadcast_to(coefs[count : count + 1, :], (rows, cols))
    for b in range(count):
        flat = coefs[b : b + 1] + coefs[GROUP + b : GROUP + b + 1] * xi
        field = field + images_ref[b] * (flat + coefs[2 * GROUP + b : 2 * GROUP + b + 1] * eta)
    out_ref[0] = science_ref[0] - field


def fill_rest(mixed_ref, science, count):
    rows = science.shape[0]
    mixed_ref[pl.ds(count, rows, stride=GROUP), :] = jnp.ones_like(science)
    mixed_ref[pl.ds(count + 1, rows, stride=GROUP), :] = science
    for spare in range(count + 2, GROUP):
        mixed_ref[pl.ds(spare, rows, stride=GROUP), :] = jnp.zeros_like(science)


def remote(source, target, send, recv, epoch, tile):
    return pltpu.make_async_remote_copy(
        src_ref=source,
        dst_ref=target,
        send_sem=send,
        recv_sem=recv,
        device_id={"epoch": epoch, "tile": tile},
        device_id_type=pl.DeviceIdType.MESH,
    )


def kernel(total, top, template_in, science_in, rowp_in, colp_in, cov_in, srow_in, scol_in, out_ref,
           science_ref, rowp_ref, colp_ref, cov_ref, srow_ref, scol_ref,
           slots, pack, edges, across_ref, parts, mine, images_ref, mixed_ref, weight_ref, profile_ref,
           row_band_ref, col_band_ref, slot_send, slot_recv, edge_send, edge_recv, part_send, part_recv, load_sem):
    count, rows, cols = images_ref.shape
    taps = rowp_ref.shape[1]
    epochs, own_rows, _ = slots.shape
    tiles = parts.shape[0]
    epoch, tile = lax.axis_index("epoch"), lax.axis_index("tile")

    loads = [
        pltpu.make_async_copy(source, target, load_sem.at[k])
        for k, (source, target) in enumerate(
            [
                (template_in, slots.at[epoch]),
                (cov_in, cov_ref),
                (srow_in, srow_ref),
                (scol_in, scol_ref),
                (rowp_in, rowp_ref),
                (colp_in, colp_ref),
                (science_in, science_ref),
            ]
        )
    ]
    for load in loads:
        load.start()
    barrier = pltpu.get_barrier_semaphore()
    for e in range(epochs):
        for t in range(tiles):
            if e or t:
                where = {"epoch": lax.rem(epoch + e, epochs), "tile": lax.rem(tile + t, tiles)}
                pl.semaphore_signal(barrier, inc=1, device_id=where, device_id_type=pl.DeviceIdType.MESH)
    loads[0].wait()
    flipped = jnp.transpose(slots[epoch])
    pack[0] = flipped[:EDGE]
    pack[1] = flipped[cols - EDGE :]
    pl.semaphore_wait(barrier, epochs * tiles - 1)

    def block_copy(e, source):
        return remote(slots.at[epoch], slots.at[source], slot_send.at[e], slot_recv.at[source],
                      lax.rem(epoch + e, epochs), tile)

    def edge_copy(e, side, source):
        beside = tile - 1 if side == 0 else tile + 1
        return remote(pack.at[side], edges.at[side, source], edge_send.at[side, e], edge_recv.at[side, source],
                      lax.rem(epoch + e, epochs), beside)

    has_left, has_right = tile > 0, tile < tiles - 1
    order = sorted(range(epochs), key=lambda e: -e * (epochs - e))
    for e in order:
        if e:
            block_copy(e, epoch).start()

        @pl.when(has_left)
        def _():
            edge_copy(e, 0, epoch).start()

        @pl.when(has_right)
        def _():
            edge_copy(e, 1, epoch).start()

    for load in loads[1:]:
        load.wait()
    make_weight(srow_ref, scol_ref, cov_ref, weight_ref)
    make_bands(rowp_ref, colp_ref, profile_ref, row_band_ref, col_band_ref, top - taps // 2)
    fill_rest(mixed_ref, science_ref[0], count)
    high = across_ref.shape[1]
    across_ref[:, :top, :] = jnp.zeros((count, top, 2 * cols), BF16)
    across_ref[:, top + rows :, :] = jnp.zeros((count, high - top - rows, 2 * cols), BF16)

    @pl.when(tile == tiles - 1)
    def _():
        edges[0] = jnp.zeros(edges.shape[1:], F32)

    @pl.when(tile == 0)
    def _():
        edges[1] = jnp.zeros(edges.shape[1:], F32)

    def arrive(source):
        e = lax.rem(epoch + epochs - source, epochs)

        @pl.when(e != 0)
        def _():
            block_copy(e, source).wait_recv()

        @pl.when(has_left)
        def _():
            edge_copy(e, 1, source).wait_recv()

        @pl.when(has_right)
        def _():
            edge_copy(e, 0, source).wait_recv()

    middle = jnp.zeros((cols - 2 * EDGE, own_rows), F32)

    def strip_of(source):
        beside = jnp.transpose(jnp.concatenate([edges[0, source], middle, edges[1, source]], axis=0))
        return jnp.concatenate([slots[source], beside], axis=1)

    groups = 2 if epochs % 2 == 0 and own_rows % 16 == 0 else 1
    each = epochs // groups
    for turn in range(groups):
        group = lax.rem(epoch // each + turn, groups)
        for k in range(each):
            arrive(group * each + k)
        strip = jnp.concatenate([strip_of(group * each + k) for k in range(each)], axis=0)
        height = each * own_rows
        at = pl.ds(pl.multiple_of(top + group * height, 16), height) if groups > 1 else pl.ds(top, height)
        column_pass(strip, at, col_band_ref, across_ref)
    row_pass(row_band_ref, across_ref, images_ref, mixed_ref)
    normal = gram(weight_ref, mixed_ref, total)
    side = 3 * GROUP
    normal = jnp.concatenate([normal, jnp.zeros((side, LANES - side), F32)], axis=1)
    mine[...] = normal

    def part_copy(t, source):
        return remote(mine, parts.at[source], part_send.at[t], part_recv.at[source],
                      epoch, lax.rem(tile + t, tiles))

    for t in range(1, tiles):
        part_copy(t, tile).start()
    for t in range(1, tiles):
        source = lax.rem(tile + tiles - t, tiles)
        part_copy(t, source).wait_recv()
        normal = normal + parts[source]
    for t in range(1, tiles):
        part_copy(t, tile).wait_send()
    for e in range(epochs):
        if e:
            block_copy(e, epoch).wait_send()

        @pl.when(has_left)
        def _():
            edge_copy(e, 0, epoch).wait_send()

        @pl.when(has_right)
        def _():
            edge_copy(e, 1, epoch).wait_send()

    coefs = solve(normal, count)
    apply(coefs, images_ref, science_ref, out_ref, total)


def local(template, science, row_profiles, col_profiles, coverage, stamp_rows, stamp_cols):
    count, taps = row_profiles.shape
    rows, cols = science.shape[1:]
    own_rows = template.shape[0]
    tiles, epochs = lax.axis_size("tile"), lax.axis_size("epoch")
    width = 2 * LANES
    top = -(-(taps // 2) // 16) * 16
    block = row_block(rows, taps - 1 + top - taps // 2, width)
    vmem = pl.BlockSpec(memory_space=pltpu.VMEM)
    dma = pltpu.SemaphoreType.DMA
    return pl.pallas_call(
        functools.partial(kernel, cols * tiles, top),
        out_shape=jax.ShapeDtypeStruct(science.shape, F32),
        in_specs=[pl.BlockSpec(memory_space=pl.ANY)] * 7,
        out_specs=vmem,
        scratch_shapes=[
            pltpu.VMEM(science.shape, F32),
            pltpu.VMEM(row_profiles.shape, F32),
            pltpu.VMEM(col_profiles.shape, F32),
            pltpu.VMEM(coverage.shape, jnp.int32),
            pltpu.VMEM((1, stamp_rows.shape[0]), jnp.int32),
            pltpu.VMEM((1, stamp_cols.shape[0]), jnp.int32),
            pltpu.VMEM((epochs, own_rows, cols), F32),
            pltpu.VMEM((2, EDGE, own_rows), F32),
            pltpu.VMEM((2, epochs, EDGE, own_rows), F32),
            pltpu.VMEM((count, rows - block + width, 2 * cols), BF16),
            pltpu.VMEM((tiles, 3 * GROUP, LANES), F32),
            pltpu.VMEM((3 * GROUP, LANES), F32),
            pltpu.VMEM((count, rows, cols), F32),
            pltpu.VMEM((rows * GROUP, cols), F32),
            pltpu.VMEM((rows * GROUP, cols), F32),
            pltpu.VMEM((2, GROUP, width), F32),
            pltpu.VMEM((2, count, block, width), BF16),
            pltpu.VMEM((2, count, cols, width), BF16),
            dma((epochs,)),
            dma((epochs,)),
            dma((2, epochs)),
            dma((2, epochs)),
            dma((tiles,)),
            dma((tiles,)),
            dma((7,)),
        ],
        compiler_params=pltpu.CompilerParams(
            collective_id=0, has_side_effects=True, vmem_limit_bytes=63 * 2**20
        ),
    )(
        template,
        science,
        row_profiles,
        col_profiles,
        coverage,
        stamp_rows.reshape(1, -1),
        stamp_cols.reshape(1, -1),
    )


def solution(mesh):
    in_specs = (
        P(("patch", "epoch"), "tile"),
        P(("patch", "epoch"), None, "tile"),
        P(),
        P(),
        P(("patch", "epoch"), "tile"),
        P(("patch", "tile")),
        P(("patch", "tile")),
    )
    out_specs = P(("patch", "epoch"), None, "tile")
    return jax.shard_map(local, mesh=mesh, in_specs=in_specs, out_specs=out_specs, check_vma=False)
```
